32 devices in a mesh: groups: 2 (over y), row: 8 (over z, x), col: 2 (over core).
Axes of the slice: x: 2, y: 2, z: 4, core: 2. Of those that a mesh axis runs over, the one named last changes fastest.
Arguments:
- gram_old: bfloat16 [28672, 14336], P(('groups', 'row'), 'col'), parts along dimension 0, may hold values from -10 to 256, as said below
- activations: bfloat16 [256, 14336], P('groups', 'row'), parts along dimension 0, may hold values from -0.5 to 0.5
- weights: float32 [14336, 512], P('row', ('groups', 'col')), parts along dimension 1, may hold values from -6 to 6
- block_mask: int32 [112, 4], P(None, 'groups'), parts along dimension 1, may hold values 0 or 1
Outputs:
- pruned: float32 [14336, 512], P('row', ('groups', 'col')), parts along dimension 1
The draws below stay inside these ranges and needn't reach their ends.
There are 2 independent parts, one for each index of `groups`. The reference program is written for one: setup_inputs(seed, part) draws one part's arguments, and reference() takes and returns one part's arrays. A program takes and returns all parts, laid end to end along the dimension named above; each array names one. Nothing has to cross between parts.
Inputs may be any that keep to these rules, and one draw needn't show every extreme that they name: `gram_old`: symmetric and positive definite.
All inputs are finite; a program needn't handle non-finite values.
Results may differ from the reference program's by a relative error of at most 0.00076.
Values may be sent and summed in bfloat16 or wider, within the bound.
A program may use at most 128 MiB of HBM per device.

```python
import math
import jax
import jax.numpy as jnp

K = 14336
BLK = 128
NCOL = 256
ROWS = 128
KB = 112
NB = 2


def draw_gram_old(key, part):
    key_noise = jax.random.fold_in(key, 11)
    key_scale = jax.random.fold_in(key, 23)
    noise = jax.random.normal(key_noise, (K, K), jnp.float32)
    symmetric = (noise + noise.T) * (1.0 / math.sqrt(2.0 * K))
    base = 3.0 * jnp.eye(K, dtype=jnp.float32) + symmetric
    position = jnp.arange(K, dtype=jnp.float32) / K
    uniform_draw = jax.random.uniform(key_scale, (K,), jnp.float32)
    squares = jnp.exp(uniform_draw * math.log(10.0)) * (1.0 + 2.0 * position)
    scales = jnp.sqrt(squares)
    return (scales[:, None] * base * scales[None, :]).astype(jnp.bfloat16)


def place_ends(values, stream_key, least, largest):
    shape = values.shape
    spot = [jax.random.randint(jax.random.fold_in(stream_key, axis), (), 0, shape[axis]) for axis in range(len(shape))]
    values = values.at[tuple(spot)].set(least)
    longest = shape.index(max(shape))
    spot[longest] = (spot[longest] + 1) % shape[longest]
    return values.at[tuple(spot)].set(largest)


def block_scale(stream_key, dims, split, smallest, largest):
    level, own = 1.0, jax.random.fold_in(stream_key, 6)
    for dim, parts in split:
        steps = jnp.exp(jax.random.uniform(jax.random.fold_in(own, dim), (parts,), jnp.float32, smallest / len(split), largest / len(split)))
        level = level * jnp.repeat(steps, dims[dim] // parts).reshape([-1 if axis == dim else 1 for axis in range(len(dims))])
    return level


def bell_draw(key, dims, deviation, limit, cuts=(), kind=jnp.bfloat16):
    factor_of = block_scale(key, dims, cuts, -0.22, 0.18) if cuts else 1.0
    result = jax.random.normal(key, dims, jnp.float32) * deviation * factor_of
    return jnp.minimum(jnp.maximum(result, -limit), limit).astype(kind)


def setup_inputs(seed: int = 0, part: int = 0) -> dict:
    splits = jax.random.split(jax.random.key(seed), 5)
    part_keys = jax.random.split(jax.random.fold_in(splits[4], part), 5)
    gram_old = draw_gram_old(jax.random.fold_in(jax.random.fold_in(splits[4], part), 71), part)
    activations = bell_draw(part_keys[1], (ROWS, K), ROWS ** -0.5, 0.5, ((1, 8),))
    weights = bell_draw(part_keys[2], (K, NCOL), 1.0, 6.0, ((0, 8), (1, 2)), jnp.float32)
    block_mask = place_ends((jax.random.randint(part_keys[3], (KB, NB), 0, 2) < 1).astype(jnp.int32), jax.random.fold_in(part_keys[3], 1), 0, 1)
    return {"gram_old": gram_old, "activations": activations, "weights": weights, "block_mask": block_mask}


damping_ratio = 0.3
epsilon = 1e-6


def expand_mask(block_mask):
    widened = jnp.repeat(block_mask.astype(jnp.float32), BLK, axis=0)
    return jnp.repeat(widened, BLK, axis=1)


def reference(gram_old, activations, weights, block_mask):
    gram_update = jnp.dot(activations.T, activations, preferred_element_type=jnp.float32)
    gram_new = (gram_old.astype(jnp.float32) + gram_update).astype(jnp.bfloat16)
    trace_total = jnp.sum(jnp.diagonal(gram_new).astype(jnp.float32))
    damping = damping_ratio * trace_total / K
    mask_full = expand_mask(block_mask)
    kept_weights = mask_full * weights
    pruned_diff = kept_weights - weights
    grad_first = jnp.dot(gram_new, pruned_diff.astype(jnp.bfloat16), preferred_element_type=jnp.float32)
    step_dir = mask_full * grad_first
    curvature = jnp.dot(gram_new, step_dir.astype(jnp.bfloat16), preferred_element_type=jnp.float32)
    masked_curve = mask_full * curvature
    grad_square = jnp.sum(step_dir * step_dir)
    grad_curve = jnp.sum(step_dir * curvature)
    curve_square = jnp.sum(masked_curve * masked_curve)
    step_first = grad_square / (grad_curve + damping * grad_square + epsilon)
    step_second = (grad_curve + damping * grad_square) / (curve_square + 2.0 * damping * grad_curve + damping * damping * grad_square + epsilon)
    grad_second = grad_first - step_first * curvature
    return kept_weights - step_first * step_dir - step_second * (mask_full * grad_second)
```

```python
import functools

import jax
import jax.numpy as jnp
from jax import lax
from jax.experimental import pallas as pl
from jax.experimental.pallas import tpu as pltpu
from jax.sharding import PartitionSpec as P

BLK = 128
CUTS = 2
LAG = 0
MESH = pl.DeviceIdType.MESH
TRANSPOSED = (((0,), (0,)), ((), ()))


damping_ratio = 0.3
epsilon = 1e-06


def partner(value, axis, distance):
    return lax.ppermute(value, axis, [(i, i ^ 1 << distance) for i in range(lax.axis_size(axis))])


def expand_local(block_mask, row_offset, row_count, col_offset, col_count):
    row_ids = (row_offset + jnp.arange(row_count, dtype=jnp.int32)) // BLK
    col_ids = (col_offset + jnp.arange(col_count, dtype=jnp.int32)) // BLK
    pick_rows = (
        row_ids[:, None] == jnp.arange(block_mask.shape[0], dtype=jnp.int32)[None, :]
    ).astype(jnp.float32)
    pick_cols = (
        col_ids[:, None] == jnp.arange(block_mask.shape[1], dtype=jnp.int32)[None, :]
    ).astype(jnp.float32)
    partial_rows = jnp.dot(
        pick_rows, block_mask.astype(jnp.float32), precision=lax.Precision.HIGHEST
    )
    return jnp.dot(partial_rows, pick_cols.T, precision=lax.Precision.HIGHEST)


def update_product(activations, inner):
    high = inner.astype(jnp.bfloat16)
    low = (inner - high.astype(jnp.float32)).astype(jnp.bfloat16)
    contract = (((0,), (0,)), ((), ()))
    return lax.dot_general(
        activations, high, contract, preferred_element_type=jnp.float32
    ) + lax.dot_general(activations, low, contract, preferred_element_type=jnp.float32)


def per_device(gram_old, activations, weights, block_mask):
    row_block = gram_old.shape[0]
    half_width = gram_old.shape[1]
    width_cols = weights.shape[1]
    row_index = lax.axis_index("row")
    col_index = lax.axis_index("col")
    row_offset = row_index * row_block
    half_offset = col_index * half_width
    diag_column = row_offset + jnp.arange(row_block, dtype=jnp.int32) - half_offset
    on_diagonal = jnp.arange(half_width, dtype=jnp.int32)[None, :] == diag_column[:, None]
    trace_part = jnp.sum(jnp.where(on_diagonal, gram_old.astype(jnp.float32), 0.0))
    acts_wide = activations.astype(jnp.float32)
    trace_part = trace_part + jnp.sum(acts_wide * acts_wide) / lax.axis_size("col")
    mask_local = expand_local(block_mask, row_offset, row_block, col_index * width_cols, width_cols)

    def apply_gram(panel):
        panel_low = panel.astype(jnp.bfloat16)
        inner = lax.psum(
            jnp.dot(activations, panel_low, preferred_element_type=jnp.float32), "row"
        )
        low_rank = update_product(activations, inner)
        column_panel = lax.all_gather(panel_low, "row", axis=0, tiled=True)
        own_half = lax.dynamic_slice_in_dim(column_panel, half_offset, half_width, 0)
        partner_need = lax.dynamic_slice_in_dim(
            column_panel, (1 - col_index) * half_width, half_width, 0
        )
        partner_half = partner(partner_need, "col", 0)
        own_part = jnp.dot(gram_old, own_half, preferred_element_type=jnp.float32)
        partner_part = jnp.dot(gram_old, partner_half, preferred_element_type=jnp.float32)
        return own_part + partner(partner_part, "col", 0) + low_rank

    kept_weights = mask_local * weights
    pruned_diff = kept_weights - weights
    grad_first = apply_gram(pruned_diff)
    step_dir = mask_local * grad_first
    curvature = apply_gram(step_dir)
    masked_curve = mask_local * curvature
    local_square = jnp.sum(step_dir * step_dir)
    local_curve = jnp.sum(step_dir * curvature)
    local_curve_square = jnp.sum(masked_curve * masked_curve)
    grad_square, grad_curve, curve_square, trace_total = lax.psum(
        jnp.stack([local_square, local_curve, local_curve_square, trace_part]), ("row", "col")
    )
    damping = damping_ratio * trace_total / (row_block * lax.axis_size("row"))
    step_first = grad_square / (grad_curve + damping * grad_square + epsilon)
    step_second = (grad_curve + damping * grad_square) / (
        curve_square + 2.0 * damping * grad_curve + damping * damping * grad_square + epsilon
    )
    grad_second = grad_first - step_first * curvature
    return kept_weights - step_first * step_dir - step_second * (mask_local * grad_second)


def fused_kernel(
    n, gram, acts, weights, mask, out,
    g_vm, own, xs, y_acc, y_rx, grad, w_vm, a_vm, a_turned, red_send, red_recv, inner, trace_row, tot, tot_a, tot_b,
    g_sem, ring_ssem, ring_rsem, par_ssem, par_rsem, y_ssem, y_rsem,
    red_ssem, red_rsem, tot_ssem, tot_rsem, sum_sem, go_sem,
):
    rows, width = weights.shape
    nb = gram.shape[1] // rows
    nz = n // 2
    chunks = CUTS
    CHUNK = rows // CUTS
    split = (chunks + 1) // 2
    last = n // 2 - 1
    blocks = rows // BLK
    members = 2 * n
    group = lax.axis_index("groups")
    row = lax.axis_index("row")
    col = lax.axis_index("col")
    me = row * 2 + col
    near_half = row // nb
    own_block = lax.rem(row, nb)

    def row_of(place):
        place = lax.rem(place + 2 * n, n)
        x = place // nz
        z = place + x * (n - 1 - 2 * place)
        return 2 * z + x

    my_z, my_x = row // 2, lax.rem(row, 2)
    place = my_z + my_x * (n - 1 - 2 * my_z)
    right, left = row_of(place + 1), row_of(place - 1)
    outer = (my_z == 0) | (my_z == nz - 1)
    z_pair = row + 2 - 4 * lax.rem(my_z, 2)
    z_middle = row + 2 * (nz - 1 - 2 * my_z)
    x_pair = row + 1 - 2 * my_x

    def mask_at(block):
        return mask[col, row * blocks + block].astype(jnp.float32)

    def source_of(way, distance):
        return row_of(place - distance) if way == 0 else row_of(place + distance)

    def chunk_span(j):
        return pl.ds(pl.multiple_of(j * CHUNK, CHUNK), CHUNK)

    def ring(part, way, hop, j):
        source = source_of(way, hop)
        there = xs.at[part, lax.rem(source, nb), chunk_span(j)]
        return pltpu.make_async_remote_copy(
            src_ref=own.at[part // 2, chunk_span(j)] if hop == 0 else there, dst_ref=there,
            send_sem=ring_ssem.at[part, way, hop, j], recv_sem=ring_rsem.at[part, way, hop, j],
            device_id=(group, right if way == 0 else left, source // nb), device_id_type=MESH,
        )

    def arrival(part, way, hop, j):
        there = xs.at[part, lax.rem(source_of(way, hop + 1), nb), chunk_span(j)]
        return pltpu.make_async_remote_copy(
            src_ref=there, dst_ref=there,
            send_sem=ring_ssem.at[part, way, hop, j], recv_sem=ring_rsem.at[part, way, hop, j],
            device_id=(group, right if way == 0 else left, col), device_id_type=MESH,
        )

    def to_partner(part, j):
        return pltpu.make_async_remote_copy(
            src_ref=own.at[part // 2, chunk_span(j)], dst_ref=xs.at[part, own_block, chunk_span(j)],
            send_sem=par_ssem.at[part, j], recv_sem=par_rsem.at[part, j],
            device_id=(group, row, 1 - col), device_id_type=MESH,
        )

    def y_copy(part, j):
        return pltpu.make_async_remote_copy(
            src_ref=y_acc.at[part, chunk_span(j)], dst_ref=y_rx.at[part // 2, chunk_span(j)],
            send_sem=y_ssem.at[part // 2, j], recv_sem=y_rsem.at[part // 2, j],
            device_id=(group, row, 1 - col), device_id_type=MESH,
        )

    def red_copy(phase, step):
        peer = (z_pair, x_pair, z_middle, z_pair)[step]
        return pltpu.make_async_remote_copy(
            src_ref=inner.at[phase, 0] if step == 1 else red_send.at[phase, step],
            dst_ref=inner.at[phase, 1] if step == 1 else red_recv.at[phase, step],
            send_sem=red_ssem.at[phase, step], recv_sem=red_rsem.at[phase, step],
            device_id=(group, peer, col), device_id_type=MESH,
        )

    def sum_copy():
        return pltpu.make_async_remote_copy(
            src_ref=tot_a, dst_ref=tot_b, send_sem=sum_sem.at[0], recv_sem=sum_sem.at[1],
            device_id=(group, row, 1), device_id_type=MESH,
        )

    def tot_copy(i):
        target = lax.rem(me + i, members)
        return pltpu.make_async_remote_copy(
            src_ref=tot.at[row], dst_ref=tot.at[row],
            send_sem=tot_ssem.at[i], recv_sem=tot_rsem.at[row],
            device_id=(group, target // 2, lax.rem(target, 2)), device_id_type=MESH,
        )

    def tot_arrival(sender):
        return pltpu.make_async_remote_copy(
            src_ref=tot.at[sender], dst_ref=tot.at[sender],
            send_sem=tot_ssem.at[0], recv_sem=tot_rsem.at[sender],
            device_id=(group, row, 1 - col), device_id_type=MESH,
        )

    def gram_copy(b):
        return pltpu.make_async_copy(
            gram.at[:, pl.ds(pl.multiple_of(b * rows, rows), rows)], g_vm.at[b], g_sem.at[b]
        )

    def here(source):
        return source // nb == col

    def launch(part, j):
        @pl.when(near_half != col)
        def _():
            to_partner(part, j).start()

        ring(part, 0, 0, j).start()
        ring(part, 1, 0, j).start()

    def start_inner(phase):
        @pl.when(outer)
        def _():
            red_copy(phase, 0).start()

    def own_inner(phase):
        value = jnp.dot(a_vm[...], own[phase], preferred_element_type=jnp.float32)
        inner[phase, 0] = value
        red_send[phase, 0] = value.astype(jnp.bfloat16)

    def reduce_inner(phase, step):
        @pl.when(jnp.logical_not(outer))
        def _():
            red_copy(phase, step).wait_recv()
            if step == 0:
                inner[phase, 0] += red_recv[phase, 0].astype(jnp.float32)
            else:
                if step == 1:
                    value = inner[phase, 0] + inner[phase, 1]
                else:
                    value = inner[phase, 2] + red_recv[phase, 2].astype(jnp.float32)
                inner[phase, 2] = value
                red_send[phase, step + 1] = value.astype(jnp.bfloat16)
            red_copy(phase, step + 1).start()

    def add_update(part):
        phase = part // 2

        @pl.when(outer)
        def _():
            red_copy(phase, 3).wait_recv()
            inner[phase, 2] = red_recv[phase, 3].astype(jnp.float32)

        value = inner[phase, 2]
        high = value.astype(jnp.bfloat16)
        low = (value - high.astype(jnp.float32)).astype(jnp.bfloat16)
        pair = jnp.concatenate([high, low], axis=1)

        @pl.loop(0, chunks)
        def _(tile):
            at = chunk_span(tile)
            both = jnp.dot(a_turned[at], pair, preferred_element_type=jnp.float32)
            y_acc[part, at] += both[:, :width] + both[:, width:]

    def multiply(part, source):
        block = lax.rem(source, nb)

        @pl.loop(0, chunks)
        def _(tile):
            at = chunk_span(tile)
            y_acc[part, at] += jnp.dot(
                g_vm[block, at], xs[part, block], preferred_element_type=jnp.float32
            )

    def multiply_both(phase, source):
        block = lax.rem(source, nb)

        @pl.loop(0, chunks)
        def _(tile):
            at = chunk_span(tile)
            panel = jnp.concatenate([xs[2 * phase, block], xs[2 * phase + 1, block]], axis=1)
            got = jnp.dot(g_vm[block, at], panel, preferred_element_type=jnp.float32)
            y_acc[2 * phase, at] += got[:, :width]
            y_acc[2 * phase + 1, at] += got[:, width:]

    def multiply_chunk(phase, source, j):
        block = lax.rem(source, nb)
        inside = pl.ds(j * CHUNK, CHUNK)

        @pl.loop(0, chunks)
        def _(tile):
            at = chunk_span(tile)
            panel = jnp.concatenate(
                [xs[2 * phase, block, inside], xs[2 * phase + 1, block, inside]], axis=1
            )
            got = jnp.dot(g_vm[block, at, inside], panel, preferred_element_type=jnp.float32)
            y_acc[2 * phase, at] += got[:, :width]
            y_acc[2 * phase + 1, at] += got[:, width:]

    def process_chunk(phase, way, hop, j):
        source = source_of(way, hop + 1)

        @pl.when(here(source))
        def _():
            multiply_chunk(phase, source, j)

    def pass_on(part, hop, j):
        for way in range(2):
            @pl.when(here(source_of(way, hop + 1)))
            def _():
                arrival(part, way, hop, j).wait_recv()
                if hop + 1 < last or (j < split) == (way == 0):
                    ring(part, way, hop + 1, j).start()

    def process(part, way, hop):
        source = source_of(way, hop + 1)

        @pl.when(here(source))
        def _():
            multiply(part, source)

    def process_both(phase, way, hop):
        source = source_of(way, hop + 1)

        @pl.when(here(source))
        def _():
            multiply_both(phase, source)

    def process_self(phase):
        @pl.when(near_half == col)
        def _():
            for j in range(chunks):
                to_partner(2 * phase + 1 - col, j).wait_recv()

            multiply_both(phase, row)

    def process_far(part):
        far = row_of(place + n // 2)

        @pl.when(here(far))
        def _():
            for j in range(chunks):
                arrival(part, 0 if j < split else 1, last, j).wait_recv()
            block = lax.rem(far, nb)

            @pl.loop(0, chunks)
            def _(j):
                at = chunk_span(j)
                y_acc[part, at] += jnp.dot(
                    g_vm[block, at], xs[part, block], preferred_element_type=jnp.float32
                )

                @pl.when(col != part % 2)
                def _():
                    y_copy(part, j).start()

        @pl.when(jnp.logical_not(here(far)) & (col != part % 2))
        def _():
            for j in range(chunks):
                y_copy(part, j).start()

    def fold(values):
        return jnp.sum(values.reshape(-1, 8, width), axis=0)

    per_chunk = CHUNK // BLK

    def put_own(phase, at, value):
        own[phase, at] = value

        @pl.when(near_half == col)
        def _():
            xs[2 * phase + col, own_block, at] = value

    def turn(part):
        for j in range(chunks):
            y_copy(part, j).wait_recv()

            @pl.loop(j * per_chunk, (j + 1) * per_chunk)
            def _(i):
                at = pl.ds(pl.multiple_of(i * BLK, BLK), BLK)
                gradient = y_acc[part, at] + y_rx[0, at]
                grad[at] = gradient
                put_own(1, at, (mask_at(i) * gradient).astype(jnp.bfloat16))

            if j == chunks - 1:
                own_inner(1)
                start_inner(1)
            launch(part + 2, j)

    def finish(part):
        def sums(i, carry):
            square, curve, curve_square = carry
            at = pl.ds(pl.multiple_of(i * BLK, BLK), BLK)
            curvature = y_acc[part, at] + y_rx[1, at]
            y_acc[part, at] = curvature
            keep = mask_at(i)
            step = keep * grad[at]
            square = square + fold(step * step)
            curve = curve + fold(step * curvature)
            curve_square = curve_square + fold((keep * curvature) * (keep * curvature))
            return square, curve, curve_square

        zero = jnp.zeros((8, width), jnp.float32)
        parts = (zero, zero, zero)
        for j in range(chunks):
            y_copy(part, j).wait_recv()
            parts = lax.fori_loop(j * per_chunk, (j + 1) * per_chunk, sums, parts)
        sums_here = tot if part == 3 else tot_a
        slot = row if part == 3 else 0
        sums_here[slot] = jnp.concatenate(
            [jnp.sum(value, axis=0, keepdims=True) for value in parts]
            + [trace_row[0:1], zero[:4]], axis=0
        )
        if part == 2:
            sum_copy().start()
        else:
            sum_copy().wait_recv()
            tot[row] += tot_b[0]
            for i in range(1, members):
                tot_copy(i).start()

    def trace():
        trace_row[...] = jnp.zeros_like(trace_row)

        @pl.when(near_half == col)
        def _():
            eye = lax.broadcasted_iota(jnp.int32, (BLK, BLK), 0) == lax.broadcasted_iota(
                jnp.int32, (BLK, BLK), 1
            )
            total = jnp.zeros((1, BLK), jnp.float32)
            for i in range(blocks):
                at = pl.ds(i * BLK, BLK)
                diagonal = jnp.where(eye, g_vm[own_block, at, at].astype(jnp.float32), 0.0)
                act = a_vm[:, at].astype(jnp.float32)
                total = total + jnp.sum(diagonal, axis=0, keepdims=True) + jnp.sum(
                    act * act, axis=0, keepdims=True
                )
            trace_row[0:1] = total

    w_copy = pltpu.make_async_copy(weights, w_vm, g_sem.at[nb])
    a_copy = pltpu.make_async_copy(acts, a_vm, g_sem.at[nb + 1])
    w_copy.start()
    a_copy.start()
    for b in range(nb):
        gram_copy(lax.rem(row + b, nb)).start()
    barrier = pltpu.get_barrier_semaphore()

    @pl.loop(1, members)
    def _(i):
        friend = lax.rem(me + i, members)
        pl.semaphore_signal(
            barrier, inc=1, device_id=(group, friend // 2, lax.rem(friend, 2)), device_id_type=MESH
        )

    w_copy.wait()
    for i in range(blocks):
        at = pl.ds(i * BLK, BLK)
        w = w_vm[at]
        put_own(0, at, (mask_at(i) * w - w).astype(jnp.bfloat16))
    a_copy.wait()
    own_inner(0)
    pl.semaphore_wait(barrier, members - 1)
    start_inner(0)

    @pl.when(col == 0)
    def _():
        for j in range(chunks):
            launch(0, j)

    y_acc[...] = jnp.zeros_like(y_acc)

    @pl.when(col == 0)
    def _():
        for j in range(chunks):
            ring(0, 0, 0, j).wait_send()
            ring(0, 1, 0, j).wait_send()
            if j == LAG:
                pl.semaphore_signal(go_sem, inc=1, device_id=(group, row, 1), device_id_type=MESH)

    @pl.when(col == 1)
    def _():
        pl.semaphore_wait(go_sem, 1)
        for j in range(chunks):
            launch(1, j)

    def owned(part, action, *rest):
        @pl.when(col == part % 2)
        def _():
            action(*rest)

    for phase in range(2):
        a, b = 2 * phase, 2 * phase + 1
        if phase == 1:
            owned(1, turn, 1)
        pass_on(a, 0, 0)
        owned(a, reduce_inner, phase, 0)
        if phase == 0:
            owned(b, reduce_inner, phase, 0)
            a_turned[...] = a_vm[...].T
        pass_on(a, 0, 1)
        owned(a, reduce_inner, phase, 1)
        pass_on(b, 0, 0)
        if phase == 0:
            for k in range(nb):
                gram_copy(lax.rem(row + k, nb)).wait()
            trace()
        else:
            owned(b, reduce_inner, phase, 0)
        pass_on(b, 0, 1)
        owned(b, reduce_inner, phase, 1)
        process_self(phase)
        pass_on(a, 1, 0)
        process_both(phase, 0, 0)
        pass_on(a, 1, 1)
        owned(a, reduce_inner, phase, 2)
        process_both(phase, 1, 0)
        pass_on(b, 1, 0)
        pass_on(b, 1, 1)
        owned(b, reduce_inner, phase, 2)
        process_both(phase, 0, 1)
        pass_on(a, 2, 0)
        process_both(phase, 1, 1)
        pass_on(a, 2, 1)
        pass_on(b, 2, 0)
        process_chunk(phase, 0, 2, 0)
        process_chunk(phase, 1, 2, 0)
        pass_on(b, 2, 1)
        owned(a, add_update, a)
        process_chunk(phase, 0, 2, 1)
        process_chunk(phase, 1, 2, 1)
        process_far(a)
        if phase == 0:
            owned(a, turn, a)
        owned(b, add_update, b)
        process_far(b)
        if phase == 1:
            owned(a, finish, a)

    owned(3, finish, 3)

    for sender in range(n):
        @pl.when((col == 0) | (row != sender))
        def _():
            tot_arrival(sender).wait_recv()

    totals = jnp.sum(jnp.sum(tot[...], axis=0), axis=1, keepdims=True)
    grad_square, grad_curve, curve_square, trace_total = (totals[i:i + 1] for i in range(4))
    damping = damping_ratio * trace_total / (n * rows)
    step_first = grad_square / (grad_curve + damping * grad_square + epsilon)
    step_second = (grad_curve + damping * grad_square) / (
        curve_square + 2.0 * damping * grad_curve + damping * damping * grad_square + epsilon
    )

    @pl.loop(0, blocks)
    def _(i):
        at = pl.ds(pl.multiple_of(i * BLK, BLK), BLK)
        keep = mask_at(i)
        gradient = grad[at]
        second = gradient - step_first * y_acc[2 + col, at]
        out[at] = keep * w_vm[at] - step_first * (keep * gradient) - step_second * (keep * second)

    for part in range(4):
        for j in range(chunks):
            @pl.when(col == part % 2)
            def _():
                if part > 0:
                    ring(part, 0, 0, j).wait_send()
                    ring(part, 1, 0, j).wait_send()

                @pl.when(near_half != col)
                def _():
                    to_partner(part, j).wait_send()

            @pl.when(col != part % 2)
            def _():
                y_copy(part, j).wait_send()

            for hop in range(1, last + 1):
                for way in range(2):
                    if hop < last or (j < split) == (way == 0):
                        @pl.when(here(source_of(way, hop)))
                        def _():
                            ring(part, way, hop, j).wait_send()
    for phase in range(2):
        @pl.when(outer)
        def _():
            red_copy(phase, 0).wait_send()

        @pl.when(jnp.logical_not(outer))
        def _():
            for step in range(1, 4):
                red_copy(phase, step).wait_send()

    @pl.when(col == 0)
    def _():
        sum_copy().wait_send()

    @pl.when(col == 1)
    def _():
        for i in range(1, members):
            tot_copy(i).wait_send()


def fused_device(gram_old, activations, weights, block_mask):
    n = lax.axis_size("row")
    rows, width = weights.shape
    depth = activations.shape[0]
    nb = gram_old.shape[1] // rows
    chunks = CUTS
    hops = n // 2
    low, wide = jnp.bfloat16, jnp.float32
    dma = pltpu.SemaphoreType.DMA
    return pl.pallas_call(
        functools.partial(fused_kernel, n),
        out_shape=jax.ShapeDtypeStruct((rows, width), wide),
        in_specs=[
            pl.BlockSpec(memory_space=pl.ANY),
            pl.BlockSpec(memory_space=pl.ANY),
            pl.BlockSpec(memory_space=pl.ANY),
            pl.BlockSpec(memory_space=pltpu.SMEM),
        ],
        out_specs=pl.BlockSpec(memory_space=pltpu.VMEM),
        scratch_shapes=[
            pltpu.VMEM((nb, rows, rows), low),
            pltpu.VMEM((2, rows, width), low),
            pltpu.VMEM((4, nb, rows, width), low),
            pltpu.VMEM((4, rows, width), wide),
            pltpu.VMEM((2, rows, width), wide),
            pltpu.VMEM((rows, width), wide),
            pltpu.VMEM((rows, width), wide),
            pltpu.VMEM((depth, rows), low),
            pltpu.VMEM((rows, depth), low),
            pltpu.VMEM((2, 4, depth, width), low),
            pltpu.VMEM((2, 4, depth, width), low),
            pltpu.VMEM((2, 3, depth, width), wide),
            pltpu.VMEM((8, width), wide),
            pltpu.VMEM((n, 8, width), wide),
            pltpu.VMEM((1, 8, width), wide),
            pltpu.VMEM((1, 8, width), wide),
            dma((nb + 2,)),
            dma((4, 2, hops, chunks)),
            dma((4, 2, hops, chunks)),
            dma((4, chunks)),
            dma((4, chunks)),
            dma((2, chunks)),
            dma((2, chunks)),
            dma((2, 4)),
            dma((2, 4)),
            dma((2 * n,)),
            dma((n,)),
            dma((2,)),
            pltpu.SemaphoreType.REGULAR,
        ],
        compiler_params=pltpu.CompilerParams(
            collective_id=0, has_side_effects=True, vmem_limit_bytes=56 * 1024 * 1024
        ),
        name="fused_steps",
    )(gram_old, activations, weights, block_mask.T)


def fits(gram_old, activations, weights, n):
    rows, width = weights.shape
    return (
        rows % (CUTS * BLK) == 0
        and width == BLK
        and n == 8
        and gram_old.shape[1] == rows * n // 2
        and activations.shape[0] % BLK == 0
        and gram_old.size <= 14 * 1024 * 1024
    )


def one_device(gram_old, activations, weights, block_mask):
    if fits(gram_old, activations, weights, lax.axis_size("row")):
        return fused_device(gram_old, activations, weights, block_mask)
    return per_device(gram_old, activations, weights, block_mask)


def solution(mesh):
    placed = (
        P(("groups", "row"), "col"),
        P("groups", "row"),
        P("row", ("groups", "col")),
        P(None, "groups"),
    )
    return jax.shard_map(
        one_device,
        mesh=mesh,
        in_specs=placed,
        out_specs=P("row", ("groups", "col")),
        check_vma=False,
    )
```

```python
import functools

import jax
import jax.numpy as jnp
from jax import lax
from jax.experimental import pallas as pl
from jax.experimental.pallas import tpu as pltpu
from jax.sharding import PartitionSpec as P

BLK = 128
CUTS = 2
MESH = pl.DeviceIdType.MESH
TRANSPOSED = (((0,), (0,)), ((), ()))


damping_ratio = 0.3
epsilon = 1e-06


def partner(value, axis, distance):
    return lax.ppermute(value, axis, [(i, i ^ 1 << distance) for i in range(lax.axis_size(axis))])


def expand_local(block_mask, row_offset, row_count, col_offset, col_count):
    row_ids = (row_offset + jnp.arange(row_count, dtype=jnp.int32)) // BLK
    col_ids = (col_offset + jnp.arange(col_count, dtype=jnp.int32)) // BLK
    pick_rows = (
        row_ids[:, None] == jnp.arange(block_mask.shape[0], dtype=jnp.int32)[None, :]
    ).astype(jnp.float32)
    pick_cols = (
        col_ids[:, None] == jnp.arange(block_mask.shape[1], dtype=jnp.int32)[None, :]
    ).astype(jnp.float32)
    partial_rows = jnp.dot(
        pick_rows, block_mask.astype(jnp.float32), precision=lax.Precision.HIGHEST
    )
    return jnp.dot(partial_rows, pick_cols.T, precision=lax.Precision.HIGHEST)


def update_product(activations, inner):
    high = inner.astype(jnp.bfloat16)
    low = (inner - high.astype(jnp.float32)).astype(jnp.bfloat16)
    contract = (((0,), (0,)), ((), ()))
    return lax.dot_general(
        activations, high, contract, preferred_element_type=jnp.float32
    ) + lax.dot_general(activations, low, contract, preferred_element_type=jnp.float32)


def per_device(gram_old, activations, weights, block_mask):
    row_block = gram_old.shape[0]
    half_width = gram_old.shape[1]
    width_cols = weights.shape[1]
    row_index = lax.axis_index("row")
    col_index = lax.axis_index("col")
    row_offset = row_index * row_block
    half_offset = col_index * half_width
    diag_column = row_offset + jnp.arange(row_block, dtype=jnp.int32) - half_offset
    on_diagonal = jnp.arange(half_width, dtype=jnp.int32)[None, :] == diag_column[:, None]
    trace_part = jnp.sum(jnp.where(on_diagonal, gram_old.astype(jnp.float32), 0.0))
    acts_wide = activations.astype(jnp.float32)
    trace_part = trace_part + jnp.sum(acts_wide * acts_wide) / lax.axis_size("col")
    mask_local = expand_local(block_mask, row_offset, row_block, col_index * width_cols, width_cols)

    def apply_gram(panel):
        panel_low = panel.astype(jnp.bfloat16)
        inner = lax.psum(
            jnp.dot(activations, panel_low, preferred_element_type=jnp.float32), "row"
        )
        low_rank = update_product(activations, inner)
        column_panel = lax.all_gather(panel_low, "row", axis=0, tiled=True)
        own_half = lax.dynamic_slice_in_dim(column_panel, half_offset, half_width, 0)
        partner_need = lax.dynamic_slice_in_dim(
            column_panel, (1 - col_index) * half_width, half_width, 0
        )
        partner_half = partner(partner_need, "col", 0)
        own_part = jnp.dot(gram_old, own_half, preferred_element_type=jnp.float32)
        partner_part = jnp.dot(gram_old, partner_half, preferred_element_type=jnp.float32)
        return own_part + partner(partner_part, "col", 0) + low_rank

    kept_weights = mask_local * weights
    pruned_diff = kept_weights - weights
    grad_first = apply_gram(pruned_diff)
    step_dir = mask_local * grad_first
    curvature = apply_gram(step_dir)
    masked_curve = mask_local * curvature
    local_square = jnp.sum(step_dir * step_dir)
    local_curve = jnp.sum(step_dir * curvature)
    local_curve_square = jnp.sum(masked_curve * masked_curve)
    grad_square, grad_curve, curve_square, trace_total = lax.psum(
        jnp.stack([local_square, local_curve, local_curve_square, trace_part]), ("row", "col")
    )
    damping = damping_ratio * trace_total / (row_block * lax.axis_size("row"))
    step_first = grad_square / (grad_curve + damping * grad_square + epsilon)
    step_second = (grad_curve + damping * grad_square) / (
        curve_square + 2.0 * damping * grad_curve + damping * damping * grad_square + epsilon
    )
    grad_second = grad_first - step_first * curvature
    return kept_weights - step_first * step_dir - step_second * (mask_local * grad_second)


def fused_kernel(
    n, gram, acts, weights, mask, out,
    g_vm, own, xs, y_acc, y_rx, grad, w_vm, a_vm, a_turned, red_send, red_recv, inner, trace_row, tot,
    g_sem, ring_ssem, ring_rsem, par_ssem, par_rsem, y_ssem, y_rsem,
    red_ssem, red_rsem, tot_sem,
):
    rows, width = weights.shape
    nb = gram.shape[1] // rows
    nz = n // 2
    chunks = CUTS
    CHUNK = rows // CUTS
    split = (chunks + 1) // 2
    last = n // 2 - 1
    blocks = rows // BLK
    members = 2 * n
    group = lax.axis_index("groups")
    row = lax.axis_index("row")
    col = lax.axis_index("col")
    me = row * 2 + col
    near_half = row // nb
    own_block = lax.rem(row, nb)

    def row_of(place):
        place = lax.rem(place + 2 * n, n)
        x = place // nz
        z = place + x * (n - 1 - 2 * place)
        return 2 * z + x

    my_z, my_x = row // 2, lax.rem(row, 2)
    place = my_z + my_x * (n - 1 - 2 * my_z)
    right, left = row_of(place + 1), row_of(place - 1)
    outer = (my_z == 0) | (my_z == nz - 1)
    z_pair = row + 2 - 4 * lax.rem(my_z, 2)
    z_middle = row + 2 * (nz - 1 - 2 * my_z)
    x_pair = row + 1 - 2 * my_x

    def mask_at(block):
        return mask[col, row * blocks + block].astype(jnp.float32)

    def source_of(way, distance):
        return row_of(place - distance) if way == 0 else row_of(place + distance)

    def chunk_span(j):
        return pl.ds(pl.multiple_of(j * CHUNK, CHUNK), CHUNK)

    def ring(part, way, hop, j):
        source = source_of(way, hop)
        there = xs.at[part, lax.rem(source, nb), chunk_span(j)]
        return pltpu.make_async_remote_copy(
            src_ref=own.at[part // 2, chunk_span(j)] if hop == 0 else there, dst_ref=there,
            send_sem=ring_ssem.at[part, way, hop], recv_sem=ring_rsem.at[part, way, hop, j],
            device_id=(group, right if way == 0 else left, source // nb), device_id_type=MESH,
        )

    def ring_sent(part, way, hop):
        source = xs.at[part, lax.rem(source_of(way, hop), nb)]
        return pltpu.make_async_remote_copy(
            src_ref=own.at[part // 2] if hop == 0 else source, dst_ref=source,
            send_sem=ring_ssem.at[part, way, hop], recv_sem=ring_rsem.at[part, way, hop, 0],
            device_id=(group, right if way == 0 else left, col), device_id_type=MESH,
        )

    def arrival(part, way, hop, j):
        there = xs.at[part, lax.rem(source_of(way, hop + 1), nb), chunk_span(j)]
        return pltpu.make_async_remote_copy(
            src_ref=there, dst_ref=there,
            send_sem=ring_ssem.at[part, way, hop], recv_sem=ring_rsem.at[part, way, hop, j],
            device_id=(group, right if way == 0 else left, col), device_id_type=MESH,
        )

    def to_partner(part, j):
        return pltpu.make_async_remote_copy(
            src_ref=own.at[part // 2, chunk_span(j)], dst_ref=xs.at[part, own_block, chunk_span(j)],
            send_sem=par_ssem.at[part, j], recv_sem=par_rsem.at[part, j],
            device_id=(group, row, 1 - col), device_id_type=MESH,
        )

    def y_copy(part, j):
        return pltpu.make_async_remote_copy(
            src_ref=y_acc.at[part, chunk_span(j)], dst_ref=y_rx.at[part // 2, chunk_span(j)],
            send_sem=y_ssem.at[part // 2, j], recv_sem=y_rsem.at[part // 2, j],
            device_id=(group, row, 1 - col), device_id_type=MESH,
        )

    def red_copy(phase, step):
        peer = (z_pair, x_pair, z_middle, z_pair)[step]
        return pltpu.make_async_remote_copy(
            src_ref=inner.at[phase, 0] if step == 1 else red_send.at[phase, step],
            dst_ref=inner.at[phase, 1] if step == 1 else red_recv.at[phase, step],
            send_sem=red_ssem.at[phase, step], recv_sem=red_rsem.at[phase, step],
            device_id=(group, peer, col), device_id_type=MESH,
        )

    def across(index, step):
        return index + (1 - 2 * lax.rem(index // 2 ** step, 2)) * 2 ** step

    def tot_copy(k):
        target = me
        for step in range(members.bit_length() - 1):
            if k >> step & 1:
                target = across(target, step)
        return pltpu.make_async_remote_copy(
            src_ref=tot.at[0], dst_ref=tot.at[k], send_sem=tot_sem.at[0], recv_sem=tot_sem.at[1],
            device_id=(group, target // 2, lax.rem(target, 2)), device_id_type=MESH,
        )

    def tot_all():
        others = tot.at[pl.ds(1, members - 1)]
        return pltpu.make_async_remote_copy(
            src_ref=others, dst_ref=others, send_sem=tot_sem.at[0], recv_sem=tot_sem.at[1],
            device_id=(group, row, 1 - col), device_id_type=MESH,
        )

    def gram_copy(b):
        return pltpu.make_async_copy(
            gram.at[:, pl.ds(pl.multiple_of(b * rows, rows), rows)], g_vm.at[b], g_sem.at[b]
        )

    def here(source):
        return source // nb == col

    def launch(part, j):
        @pl.when(near_half != col)
        def _():
            to_partner(part, j).start()

        ring(part, 0, 0, j).start()
        ring(part, 1, 0, j).start()

    def start_inner(phase):
        @pl.when(outer)
        def _():
            red_copy(phase, 0).start()

    def own_inner(phase):
        value = jnp.dot(a_vm[...], own[phase], preferred_element_type=jnp.float32)
        inner[phase, 0] = value
        red_send[phase, 0] = value.astype(jnp.bfloat16)

    def reduce_inner(phase, step):
        @pl.when(jnp.logical_not(outer))
        def _():
            red_copy(phase, step).wait_recv()
            if step == 0:
                inner[phase, 0] += red_recv[phase, 0].astype(jnp.float32)
            else:
                if step == 1:
                    value = inner[phase, 0] + inner[phase, 1]
                else:
                    value = inner[phase, 2] + red_recv[phase, 2].astype(jnp.float32)
                inner[phase, 2] = value
                red_send[phase, step + 1] = value.astype(jnp.bfloat16)
            red_copy(phase, step + 1).start()

    def add_update(part):
        phase = part // 2

        @pl.when(outer)
        def _():
            red_copy(phase, 3).wait_recv()
            inner[phase, 2] = red_recv[phase, 3].astype(jnp.float32)

        value = inner[phase, 2]
        high = value.astype(jnp.bfloat16)
        low = (value - high.astype(jnp.float32)).astype(jnp.bfloat16)
        pair = jnp.concatenate([high, low], axis=1)

        @pl.loop(0, chunks)
        def _(tile):
            at = chunk_span(tile)
            both = jnp.dot(a_turned[at], pair, preferred_element_type=jnp.float32)
            y_acc[part, at] += both[:, :width] + both[:, width:]

    def multiply(part, source):
        block = lax.rem(source, nb)

        @pl.loop(0, chunks)
        def _(tile):
            at = chunk_span(tile)
            y_acc[part, at] += jnp.dot(
                g_vm[block, at], xs[part, block], preferred_element_type=jnp.float32
            )

    def multiply_both(phase, source):
        block = lax.rem(source, nb)

        @pl.loop(0, chunks)
        def _(tile):
            at = chunk_span(tile)
            panel = jnp.concatenate([xs[2 * phase, block], xs[2 * phase + 1, block]], axis=1)
            got = jnp.dot(g_vm[block, at], panel, preferred_element_type=jnp.float32)
            y_acc[2 * phase, at] += got[:, :width]
            y_acc[2 * phase + 1, at] += got[:, width:]

    def multiply_chunk(phase, source, j):
        block = lax.rem(source, nb)
        inside = pl.ds(j * CHUNK, CHUNK)

        @pl.loop(0, chunks)
        def _(tile):
            at = chunk_span(tile)
            panel = jnp.concatenate(
                [xs[2 * phase, block, inside], xs[2 * phase + 1, block, inside]], axis=1
            )
            got = jnp.dot(g_vm[block, at, inside], panel, preferred_element_type=jnp.float32)
            y_acc[2 * phase, at] += got[:, :width]
            y_acc[2 * phase + 1, at] += got[:, width:]

    def process_chunk(phase, way, hop, j):
        source = source_of(way, hop + 1)

        @pl.when(here(source))
        def _():
            multiply_chunk(phase, source, j)

    def pass_on(part, hop, j):
        for way in range(2):
            @pl.when(here(source_of(way, hop + 1)))
            def _():
                arrival(part, way, hop, j).wait_recv()
                if hop + 1 < last or (j < split) == (way == 0):
                    ring(part, way, hop + 1, j).start()

    def process(part, way, hop):
        source = source_of(way, hop + 1)

        @pl.when(here(source))
        def _():
            multiply(part, source)

    def process_both(phase, way, hop):
        source = source_of(way, hop + 1)

        @pl.when(here(source))
        def _():
            multiply_both(phase, source)

    def process_self(phase):
        @pl.when(near_half == col)
        def _():
            for j in range(chunks):
                to_partner(2 * phase + 1 - col, j).wait_recv()

            multiply_both(phase, row)

    def process_far(part):
        far = row_of(place + n // 2)

        @pl.when(here(far))
        def _():
            for j in range(chunks):
                arrival(part, 0 if j < split else 1, last, j).wait_recv()
            block = lax.rem(far, nb)

            @pl.loop(0, chunks)
            def _(j):
                at = chunk_span(j)
                y_acc[part, at] += jnp.dot(
                    g_vm[block, at], xs[part, block], preferred_element_type=jnp.float32
                )

                @pl.when(col != part % 2)
                def _():
                    y_copy(part, j).start()

        @pl.when(jnp.logical_not(here(far)) & (col != part % 2))
        def _():
            for j in range(chunks):
                y_copy(part, j).start()

    def fold(values):
        return jnp.sum(values.reshape(-1, 8, width), axis=0)

    per_chunk = CHUNK // BLK

    def put_own(phase, at, value):
        own[phase, at] = value

        @pl.when(near_half == col)
        def _():
            xs[2 * phase + col, own_block, at] = value

    def turn(part):
        for j in range(chunks):
            y_copy(part, j).wait_recv()

            @pl.loop(j * per_chunk, (j + 1) * per_chunk)
            def _(i):
                at = pl.ds(pl.multiple_of(i * BLK, BLK), BLK)
                gradient = y_acc[part, at] + y_rx[0, at]
                grad[at] = gradient
                put_own(1, at, (mask_at(i) * gradient).astype(jnp.bfloat16))

            if j == chunks - 1:
                own_inner(1)
                start_inner(1)
            launch(part + 2, j)

    def finish(part):
        def sums(i, carry):
            square, curve, curve_square = carry
            at = pl.ds(pl.multiple_of(i * BLK, BLK), BLK)
            curvature = y_acc[part, at] + y_rx[1, at]
            y_acc[part, at] = curvature
            keep = mask_at(i)
            step = keep * grad[at]
            square = square + fold(step * step)
            curve = curve + fold(step * curvature)
            curve_square = curve_square + fold((keep * curvature) * (keep * curvature))
            return square, curve, curve_square

        zero = jnp.zeros((8, width), jnp.float32)
        parts = (zero, zero, zero)
        for j in range(chunks):
            y_copy(part, j).wait_recv()
            parts = lax.fori_loop(j * per_chunk, (j + 1) * per_chunk, sums, parts)
        tot[0] = jnp.concatenate(
            [jnp.sum(value, axis=0, keepdims=True) for value in parts]
            + [trace_row[0:1], zero[:4]], axis=0
        )
        for k in reversed(range(1, members)):
            tot_copy(k).start()

    def trace():
        trace_row[...] = jnp.zeros_like(trace_row)

        @pl.when(near_half == col)
        def _():
            eye = lax.broadcasted_iota(jnp.int32, (BLK, BLK), 0) == lax.broadcasted_iota(
                jnp.int32, (BLK, BLK), 1
            )
            total = jnp.zeros((1, BLK), jnp.float32)
            for i in range(blocks):
                at = pl.ds(i * BLK, BLK)
                diagonal = jnp.where(eye, g_vm[own_block, at, at].astype(jnp.float32), 0.0)
                act = a_vm[:, at].astype(jnp.float32)
                total = total + jnp.sum(diagonal, axis=0, keepdims=True) + jnp.sum(
                    act * act, axis=0, keepdims=True
                )
            trace_row[0:1] = total

    w_copy = pltpu.make_async_copy(weights, w_vm, g_sem.at[nb])
    a_copy = pltpu.make_async_copy(acts, a_vm, g_sem.at[nb + 1])
    w_copy.start()
    a_copy.start()
    for b in range(nb):
        gram_copy(lax.rem(row + b, nb)).start()
    barrier = pltpu.get_barrier_semaphore()

    @pl.loop(1, members)
    def _(i):
        friend = lax.rem(me + i, members)
        pl.semaphore_signal(
            barrier, inc=1, device_id=(group, friend // 2, lax.rem(friend, 2)), device_id_type=MESH
        )

    w_copy.wait()
    for i in range(blocks):
        at = pl.ds(i * BLK, BLK)
        w = w_vm[at]
        put_own(0, at, (mask_at(i) * w - w).astype(jnp.bfloat16))
    a_copy.wait()
    own_inner(0)
    pl.semaphore_wait(barrier, members - 1)
    start_inner(0)

    @pl.when(col == 0)
    def _():
        for j in range(chunks):
            launch(0, j)

    y_acc[...] = jnp.zeros_like(y_acc)

    @pl.when(col == 1)
    def _():
        for j in range(chunks):
            launch(1, j)

    def owned(part, action, *rest):
        @pl.when(col == part % 2)
        def _():
            action(*rest)

    for phase in range(2):
        a, b = 2 * phase, 2 * phase + 1
        if phase == 1:
            owned(1, turn, 1)
        pass_on(a, 0, 0)
        owned(a, reduce_inner, phase, 0)
        if phase == 0:
            owned(b, reduce_inner, phase, 0)
            a_turned[...] = a_vm[...].T
        pass_on(a, 0, 1)
        owned(a, reduce_inner, phase, 1)
        pass_on(b, 0, 0)
        if phase == 0:
            for k in range(nb):
                gram_copy(lax.rem(row + k, nb)).wait()
            trace()
        else:
            owned(b, reduce_inner, phase, 0)
        pass_on(b, 0, 1)
        owned(b, reduce_inner, phase, 1)
        process_self(phase)
        pass_on(a, 1, 0)
        process_both(phase, 0, 0)
        pass_on(a, 1, 1)
        owned(a, reduce_inner, phase, 2)
        process_both(phase, 1, 0)
        pass_on(b, 1, 0)
        pass_on(b, 1, 1)
        owned(b, reduce_inner, phase, 2)
        process_both(phase, 0, 1)
        pass_on(a, 2, 0)
        process_both(phase, 1, 1)
        pass_on(a, 2, 1)
        pass_on(b, 2, 0)
        process_chunk(phase, 0, 2, 0)
        process_chunk(phase, 1, 2, 0)
        pass_on(b, 2, 1)
        owned(a, add_update, a)
        process_chunk(phase, 0, 2, 1)
        process_chunk(phase, 1, 2, 1)
        process_far(a)
        if phase == 0:
            owned(a, turn, a)
        owned(b, add_update, b)
        process_far(b)
        if phase == 1:
            owned(a, finish, a)

    owned(3, finish, 3)

    tot_all().wait_recv()

    totals = jnp.sum(jnp.sum(tot[...], axis=0), axis=1, keepdims=True)
    grad_square, grad_curve, curve_square, trace_total = (totals[i:i + 1] for i in range(4))
    damping = damping_ratio * trace_total / (n * rows)
    step_first = grad_square / (grad_curve + damping * grad_square + epsilon)
    step_second = (grad_curve + damping * grad_square) / (
        curve_square + 2.0 * damping * grad_curve + damping * damping * grad_square + epsilon
    )

    shape = (BLK, width)
    first = jnp.broadcast_to(step_first, shape)
    second = jnp.broadcast_to(step_second, shape)

    @pl.loop(0, blocks)
    def _(i):
        at = pl.ds(pl.multiple_of(i * BLK, BLK), BLK)
        gradient = grad[at]
        moved = w_vm[at] - first * gradient - second * (gradient - first * y_acc[2 + col, at])
        out[at] = mask_at(i) * moved

    for part in range(4):
        @pl.when(col == part % 2)
        def _():
            ring_sent(part, 0, 0).wait_send()
            ring_sent(part, 1, 0).wait_send()

            @pl.when(near_half != col)
            def _():
                for j in range(chunks):
                    to_partner(part, j).wait_send()

        @pl.when(col != part % 2)
        def _():
            for j in range(chunks):
                y_copy(part, j).wait_send()

        for way in range(2):
            for hop in range(1, last + 1):
                @pl.when(here(source_of(way, hop)))
                def _():
                    if hop < last:
                        ring_sent(part, way, hop).wait_send()
                    else:
                        for j in range(chunks):
                            if (j < split) == (way == 0):
                                ring(part, way, hop, j).wait_send()
    for phase in range(2):
        @pl.when(outer)
        def _():
            red_copy(phase, 0).wait_send()

        @pl.when(jnp.logical_not(outer))
        def _():
            for step in range(1, 4):
                red_copy(phase, step).wait_send()

    tot_all().wait_send()


def fused_device(gram_old, activations, weights, block_mask):
    n = lax.axis_size("row")
    rows, width = weights.shape
    depth = activations.shape[0]
    nb = gram_old.shape[1] // rows
    chunks = CUTS
    hops = n // 2
    low, wide = jnp.bfloat16, jnp.float32
    dma = pltpu.SemaphoreType.DMA
    return pl.pallas_call(
        functools.partial(fused_kernel, n),
        out_shape=jax.ShapeDtypeStruct((rows, width), wide),
        in_specs=[
            pl.BlockSpec(memory_space=pl.ANY),
            pl.BlockSpec(memory_space=pl.ANY),
            pl.BlockSpec(memory_space=pl.ANY),
            pl.BlockSpec(memory_space=pltpu.SMEM),
        ],
        out_specs=pl.BlockSpec(memory_space=pltpu.VMEM),
        scratch_shapes=[
            pltpu.VMEM((nb, rows, rows), low),
            pltpu.VMEM((2, rows, width), low),
            pltpu.VMEM((4, nb, rows, width), low),
            pltpu.VMEM((4, rows, width), wide),
            pltpu.VMEM((2, rows, width), wide),
            pltpu.VMEM((rows, width), wide),
            pltpu.VMEM((rows, width), wide),
            pltpu.VMEM((depth, rows), low),
            pltpu.VMEM((rows, depth), low),
            pltpu.VMEM((2, 4, depth, width), low),
            pltpu.VMEM((2, 4, depth, width), low),
            pltpu.VMEM((2, 3, depth, width), wide),
            pltpu.VMEM((8, width), wide),
            pltpu.VMEM((2 * n, 8, width), wide),
            dma((nb + 2,)),
            dma((4, 2, hops)),
            dma((4, 2, hops, chunks)),
            dma((4, chunks)),
            dma((4, chunks)),
            dma((2, chunks)),
            dma((2, chunks)),
            dma((2, 4)),
            dma((2, 4)),
            dma((2,)),
        ],
        compiler_params=pltpu.CompilerParams(
            collective_id=0, has_side_effects=True, vmem_limit_bytes=56 * 1024 * 1024
        ),
        name="fused_steps",
    )(gram_old, activations, weights, block_mask.T)


def fits(gram_old, activations, weights, n):
    rows, width = weights.shape
    return (
        rows % (CUTS * BLK) == 0
        and width == BLK
        and n == 8
        and gram_old.shape[1] == rows * n // 2
        and activations.shape[0] % BLK == 0
        and gram_old.size <= 14 * 1024 * 1024
    )


def one_device(gram_old, activations, weights, block_mask):
    if fits(gram_old, activations, weights, lax.axis_size("row")):
        return fused_device(gram_old, activations, weights, block_mask)
    return per_device(gram_old, activations, weights, block_mask)


def solution(mesh):
    placed = (
        P(("groups", "row"), "col"),
        P("groups", "row"),
        P("row", ("groups", "col")),
        P(None, "groups"),
    )
    return jax.shard_map(
        one_device,
        mesh=mesh,
        in_specs=placed,
        out_specs=P("row", ("groups", "col")),
        check_vma=False,
    )
```

```python
import functools

import jax
import jax.numpy as jnp
from jax import lax
from jax.experimental import pallas as pl
from jax.experimental.pallas import tpu as pltpu
from jax.sharding import PartitionSpec as P

BLK = 128
CUTS = 2
MESH = pl.DeviceIdType.MESH
TRANSPOSED = (((0,), (0,)), ((), ()))


damping_ratio = 0.3
epsilon = 1e-06


def partner(value, axis, distance):
    return lax.ppermute(value, axis, [(i, i ^ 1 << distance) for i in range(lax.axis_size(axis))])


def expand_local(block_mask, row_offset, row_count, col_offset, col_count):
    row_ids = (row_offset + jnp.arange(row_count, dtype=jnp.int32)) // BLK
    col_ids = (col_offset + jnp.arange(col_count, dtype=jnp.int32)) // BLK
    pick_rows = (
        row_ids[:, None] == jnp.arange(block_mask.shape[0], dtype=jnp.int32)[None, :]
    ).astype(jnp.float32)
    pick_cols = (
        col_ids[:, None] == jnp.arange(block_mask.shape[1], dtype=jnp.int32)[None, :]
    ).astype(jnp.float32)
    partial_rows = jnp.dot(
        pick_rows, block_mask.astype(jnp.float32), precision=lax.Precision.HIGHEST
    )
    return jnp.dot(partial_rows, pick_cols.T, precision=lax.Precision.HIGHEST)


def update_product(activations, inner):
    high = inner.astype(jnp.bfloat16)
    low = (inner - high.astype(jnp.float32)).astype(jnp.bfloat16)
    contract = (((0,), (0,)), ((), ()))
    return lax.dot_general(
        activations, high, contract, preferred_element_type=jnp.float32
    ) + lax.dot_general(activations, low, contract, preferred_element_type=jnp.float32)


def per_device(gram_old, activations, weights, block_mask):
    row_block = gram_old.shape[0]
    half_width = gram_old.shape[1]
    width_cols = weights.shape[1]
    row_index = lax.axis_index("row")
    col_index = lax.axis_index("col")
    row_offset = row_index * row_block
    half_offset = col_index * half_width
    diag_column = row_offset + jnp.arange(row_block, dtype=jnp.int32) - half_offset
    on_diagonal = jnp.arange(half_width, dtype=jnp.int32)[None, :] == diag_column[:, None]
    trace_part = jnp.sum(jnp.where(on_diagonal, gram_old.astype(jnp.float32), 0.0))
    acts_wide = activations.astype(jnp.float32)
    trace_part = trace_part + jnp.sum(acts_wide * acts_wide) / lax.axis_size("col")
    mask_local = expand_local(block_mask, row_offset, row_block, col_index * width_cols, width_cols)

    def apply_gram(panel):
        panel_low = panel.astype(jnp.bfloat16)
        inner = lax.psum(
            jnp.dot(activations, panel_low, preferred_element_type=jnp.float32), "row"
        )
        low_rank = update_product(activations, inner)
        column_panel = lax.all_gather(panel_low, "row", axis=0, tiled=True)
        own_half = lax.dynamic_slice_in_dim(column_panel, half_offset, half_width, 0)
        partner_need = lax.dynamic_slice_in_dim(
            column_panel, (1 - col_index) * half_width, half_width, 0
        )
        partner_half = partner(partner_need, "col", 0)
        own_part = jnp.dot(gram_old, own_half, preferred_element_type=jnp.float32)
        partner_part = jnp.dot(gram_old, partner_half, preferred_element_type=jnp.float32)
        return own_part + partner(partner_part, "col", 0) + low_rank

    kept_weights = mask_local * weights
    pruned_diff = kept_weights - weights
    grad_first = apply_gram(pruned_diff)
    step_dir = mask_local * grad_first
    curvature = apply_gram(step_dir)
    masked_curve = mask_local * curvature
    local_square = jnp.sum(step_dir * step_dir)
    local_curve = jnp.sum(step_dir * curvature)
    local_curve_square = jnp.sum(masked_curve * masked_curve)
    grad_square, grad_curve, curve_square, trace_total = lax.psum(
        jnp.stack([local_square, local_curve, local_curve_square, trace_part]), ("row", "col")
    )
    damping = damping_ratio * trace_total / (row_block * lax.axis_size("row"))
    step_first = grad_square / (grad_curve + damping * grad_square + epsilon)
    step_second = (grad_curve + damping * grad_square) / (
        curve_square + 2.0 * damping * grad_curve + damping * damping * grad_square + epsilon
    )
    grad_second = grad_first - step_first * curvature
    return kept_weights - step_first * step_dir - step_second * (mask_local * grad_second)


def fused_kernel(
    n, gram, acts, weights, mask, out,
    g_vm, own, xs, y_acc, y_rx, grad, w_vm, a_vm, a_turned, red_send, red_recv, inner, trace_row, tot,
    g_sem, ring_ssem, ring_rsem, par_ssem, par_rsem, y_ssem, y_rsem,
    red_ssem, red_rsem, tot_sem,
):
    rows, width = weights.shape
    nb = gram.shape[1] // rows
    nz = n // 2
    chunks = CUTS
    CHUNK = rows // CUTS
    split = (chunks + 1) // 2
    last = n // 2 - 1
    blocks = rows // BLK
    members = 2 * n
    group = lax.axis_index("groups")
    row = lax.axis_index("row")
    col = lax.axis_index("col")
    me = row * 2 + col
    near_half = row // nb
    own_block = lax.rem(row, nb)

    def row_of(place):
        place = lax.rem(place + 2 * n, n)
        x = place // nz
        z = place + x * (n - 1 - 2 * place)
        return 2 * z + x

    my_z, my_x = row // 2, lax.rem(row, 2)
    place = my_z + my_x * (n - 1 - 2 * my_z)
    right, left = row_of(place + 1), row_of(place - 1)
    outer = (my_z == 0) | (my_z == nz - 1)
    z_pair = row + 2 - 4 * lax.rem(my_z, 2)
    z_middle = row + 2 * (nz - 1 - 2 * my_z)
    x_pair = row + 1 - 2 * my_x

    def mask_at(block):
        return mask[col, row * blocks + block].astype(jnp.float32)

    def source_of(way, distance):
        return row_of(place - distance) if way == 0 else row_of(place + distance)

    def chunk_span(j):
        return pl.ds(pl.multiple_of(j * CHUNK, CHUNK), CHUNK)

    def ring(part, way, hop, j):
        source = source_of(way, hop)
        there = xs.at[part, lax.rem(source, nb), chunk_span(j)]
        return pltpu.make_async_remote_copy(
            src_ref=own.at[part // 2, chunk_span(j)] if hop == 0 else there, dst_ref=there,
            send_sem=ring_ssem.at[part, way, hop], recv_sem=ring_rsem.at[part, way, hop, j],
            device_id=(group, right if way == 0 else left, source // nb), device_id_type=MESH,
        )

    def ring_sent(part, way, hop):
        source = xs.at[part, lax.rem(source_of(way, hop), nb)]
        return pltpu.make_async_remote_copy(
            src_ref=own.at[part // 2] if hop == 0 else source, dst_ref=source,
            send_sem=ring_ssem.at[part, way, hop], recv_sem=ring_rsem.at[part, way, hop, 0],
            device_id=(group, right if way == 0 else left, col), device_id_type=MESH,
        )

    def arrival(part, way, hop, j):
        there = xs.at[part, lax.rem(source_of(way, hop + 1), nb), chunk_span(j)]
        return pltpu.make_async_remote_copy(
            src_ref=there, dst_ref=there,
            send_sem=ring_ssem.at[part, way, hop], recv_sem=ring_rsem.at[part, way, hop, j],
            device_id=(group, right if way == 0 else left, col), device_id_type=MESH,
        )

    def to_partner(part, j):
        return pltpu.make_async_remote_copy(
            src_ref=own.at[part // 2, chunk_span(j)], dst_ref=xs.at[part, own_block, chunk_span(j)],
            send_sem=par_ssem.at[part, j], recv_sem=par_rsem.at[part, j],
            device_id=(group, row, 1 - col), device_id_type=MESH,
        )

    def y_copy(part, j):
        return pltpu.make_async_remote_copy(
            src_ref=y_acc.at[part, chunk_span(j)], dst_ref=y_rx.at[part // 2, chunk_span(j)],
            send_sem=y_ssem.at[part // 2, j], recv_sem=y_rsem.at[part // 2, j],
            device_id=(group, row, 1 - col), device_id_type=MESH,
        )

    def red_copy(phase, step):
        peer = (z_pair, x_pair, z_middle, z_pair)[step]
        return pltpu.make_async_remote_copy(
            src_ref=inner.at[phase, 0] if step == 1 else red_send.at[phase, step],
            dst_ref=inner.at[phase, 1] if step == 1 else red_recv.at[phase, step],
            send_sem=red_ssem.at[phase, step], recv_sem=red_rsem.at[phase, step],
            device_id=(group, peer, col), device_id_type=MESH,
        )

    def across(index, step):
        return index + (1 - 2 * lax.rem(index // 2 ** step, 2)) * 2 ** step

    def tot_copy(k):
        target = me
        for step in range(members.bit_length() - 1):
            if k >> step & 1:
                target = across(target, step)
        return pltpu.make_async_remote_copy(
            src_ref=tot.at[0], dst_ref=tot.at[k], send_sem=tot_sem.at[0], recv_sem=tot_sem.at[1],
            device_id=(group, target // 2, lax.rem(target, 2)), device_id_type=MESH,
        )

    def tot_all():
        others = tot.at[pl.ds(1, members - 1)]
        return pltpu.make_async_remote_copy(
            src_ref=others, dst_ref=others, send_sem=tot_sem.at[0], recv_sem=tot_sem.at[1],
            device_id=(group, row, 1 - col), device_id_type=MESH,
        )

    def gram_copy(b):
        return pltpu.make_async_copy(
            gram.at[:, pl.ds(pl.multiple_of(b * rows, rows), rows)], g_vm.at[b], g_sem.at[b]
        )

    def here(source):
        return source // nb == col

    def launch(part, j):
        @pl.when(near_half != col)
        def _():
            to_partner(part, j).start()

        ring(part, 0, 0, j).start()
        ring(part, 1, 0, j).start()

    def start_inner(phase):
        @pl.when(outer)
        def _():
            red_copy(phase, 0).start()

    def own_inner(phase):
        value = jnp.dot(a_vm[...], own[phase], preferred_element_type=jnp.float32)
        inner[phase, 0] = value
        red_send[phase, 0] = value.astype(jnp.bfloat16)

    def reduce_inner(phase, step):
        @pl.when(jnp.logical_not(outer))
        def _():
            red_copy(phase, step).wait_recv()
            if step == 0:
                inner[phase, 0] += red_recv[phase, 0].astype(jnp.float32)
            else:
                if step == 1:
                    value = inner[phase, 0] + inner[phase, 1]
                else:
                    value = inner[phase, 2] + red_recv[phase, 2].astype(jnp.float32)
                inner[phase, 2] = value
                red_send[phase, step + 1] = value.astype(jnp.bfloat16)
            red_copy(phase, step + 1).start()

    def add_update(part):
        phase = part // 2

        @pl.when(outer)
        def _():
            red_copy(phase, 3).wait_recv()
            inner[phase, 2] = red_recv[phase, 3].astype(jnp.float32)

        value = inner[phase, 2]
        high = value.astype(jnp.bfloat16)
        low = (value - high.astype(jnp.float32)).astype(jnp.bfloat16)
        pair = jnp.concatenate([high, low], axis=1)

        @pl.loop(0, chunks)
        def _(tile):
            at = chunk_span(tile)
            both = jnp.dot(a_turned[at], pair, preferred_element_type=jnp.float32)
            y_acc[part, at] += both[:, :width] + both[:, width:]

    def multiply(part, source):
        block = lax.rem(source, nb)

        @pl.loop(0, chunks)
        def _(tile):
            at = chunk_span(tile)
            y_acc[part, at] += jnp.dot(
                g_vm[block, at], xs[part, block], preferred_element_type=jnp.float32
            )

    def multiply_both(phase, source):
        block = lax.rem(source, nb)

        @pl.loop(0, chunks)
        def _(tile):
            at = chunk_span(tile)
            panel = jnp.concatenate([xs[2 * phase, block], xs[2 * phase + 1, block]], axis=1)
            got = jnp.dot(g_vm[block, at], panel, preferred_element_type=jnp.float32)
            y_acc[2 * phase, at] += got[:, :width]
            y_acc[2 * phase + 1, at] += got[:, width:]

    def multiply_chunk(phase, source, j):
        block = lax.rem(source, nb)
        inside = pl.ds(j * CHUNK, CHUNK)

        @pl.loop(0, chunks)
        def _(tile):
            at = chunk_span(tile)
            panel = jnp.concatenate(
                [xs[2 * phase, block, inside], xs[2 * phase + 1, block, inside]], axis=1
            )
            got = jnp.dot(g_vm[block, at, inside], panel, preferred_element_type=jnp.float32)
            y_acc[2 * phase, at] += got[:, :width]
            y_acc[2 * phase + 1, at] += got[:, width:]

    def process_chunk(phase, way, hop, j):
        source = source_of(way, hop + 1)

        @pl.when(here(source))
        def _():
            multiply_chunk(phase, source, j)

    def pass_on(part, hop, j):
        for way in range(2):
            @pl.when(here(source_of(way, hop + 1)))
            def _():
                arrival(part, way, hop, j).wait_recv()
                if hop + 1 < last or (j < split) == (way == 0):
                    ring(part, way, hop + 1, j).start()

    def process(part, way, hop):
        source = source_of(way, hop + 1)

        @pl.when(here(source))
        def _():
            multiply(part, source)

    def process_both(phase, way, hop):
        source = source_of(way, hop + 1)

        @pl.when(here(source))
        def _():
            multiply_both(phase, source)

    def process_self(phase):
        @pl.when(near_half == col)
        def _():
            for j in range(chunks):
                to_partner(2 * phase + 1 - col, j).wait_recv()

            multiply_both(phase, row)

    def process_far(part):
        far = row_of(place + n // 2)

        @pl.when(here(far))
        def _():
            for j in range(chunks):
                arrival(part, 0 if j < split else 1, last, j).wait_recv()
            block = lax.rem(far, nb)

            @pl.loop(0, chunks)
            def _(j):
                at = chunk_span(j)
                y_acc[part, at] += jnp.dot(
                    g_vm[block, at], xs[part, block], preferred_element_type=jnp.float32
                )

                @pl.when(col != part % 2)
                def _():
                    y_copy(part, j).start()

        @pl.when(jnp.logical_not(here(far)) & (col != part % 2))
        def _():
            for j in range(chunks):
                y_copy(part, j).start()

    def process_far_both(phase):
        far = row_of(place + n // 2)
        block = lax.rem(far, nb)

        def send(tile):
            for panel in range(2):
                @pl.when(col != panel)
                def _():
                    y_copy(2 * phase + panel, tile).start()

        @pl.when(here(far))
        def _():
            for part in (2 * phase, 2 * phase + 1):
                for j in range(chunks):
                    arrival(part, 0 if j < split else 1, last, j).wait_recv()

            @pl.loop(0, chunks)
            def _(tile):
                at = chunk_span(tile)
                panel = jnp.concatenate([xs[2 * phase, block], xs[2 * phase + 1, block]], axis=1)
                got = jnp.dot(g_vm[block, at], panel, preferred_element_type=jnp.float32)
                y_acc[2 * phase, at] += got[:, :width]
                y_acc[2 * phase + 1, at] += got[:, width:]
                send(tile)

        @pl.when(jnp.logical_not(here(far)))
        def _():
            for j in range(chunks):
                send(j)

    def fold(values):
        return jnp.sum(values.reshape(-1, 8, width), axis=0)

    per_chunk = CHUNK // BLK

    def put_own(phase, at, value):
        own[phase, at] = value

        @pl.when(near_half == col)
        def _():
            xs[2 * phase + col, own_block, at] = value

    def turn(part):
        for j in range(chunks):
            y_copy(part, j).wait_recv()

            @pl.loop(j * per_chunk, (j + 1) * per_chunk)
            def _(i):
                at = pl.ds(pl.multiple_of(i * BLK, BLK), BLK)
                gradient = y_acc[part, at] + y_rx[0, at]
                grad[at] = gradient
                put_own(1, at, (mask_at(i) * gradient).astype(jnp.bfloat16))

            if j == chunks - 1:
                own_inner(1)
                start_inner(1)
            launch(part + 2, j)

    def finish(part):
        def sums(i, carry):
            square, curve, curve_square = carry
            at = pl.ds(pl.multiple_of(i * BLK, BLK), BLK)
            curvature = y_acc[part, at] + y_rx[1, at]
            y_acc[part, at] = curvature
            keep = mask_at(i)
            step = keep * grad[at]
            square = square + fold(step * step)
            curve = curve + fold(step * curvature)
            curve_square = curve_square + fold((keep * curvature) * (keep * curvature))
            return square, curve, curve_square

        zero = jnp.zeros((8, width), jnp.float32)
        parts = (zero, zero, zero)
        for j in range(chunks):
            y_copy(part, j).wait_recv()
            parts = lax.fori_loop(j * per_chunk, (j + 1) * per_chunk, sums, parts)
        tot[0] = jnp.concatenate(
            [jnp.sum(value, axis=0, keepdims=True) for value in parts]
            + [trace_row[0:1], zero[:4]], axis=0
        )
        for k in reversed(range(1, members)):
            tot_copy(k).start()

    def trace():
        trace_row[...] = jnp.zeros_like(trace_row)

        @pl.when(near_half == col)
        def _():
            eye = lax.broadcasted_iota(jnp.int32, (BLK, BLK), 0) == lax.broadcasted_iota(
                jnp.int32, (BLK, BLK), 1
            )
            total = jnp.zeros((1, BLK), jnp.float32)
            for i in range(blocks):
                at = pl.ds(i * BLK, BLK)
                diagonal = jnp.where(eye, g_vm[own_block, at, at].astype(jnp.float32), 0.0)
                act = a_vm[:, at].astype(jnp.float32)
                total = total + jnp.sum(diagonal, axis=0, keepdims=True) + jnp.sum(
                    act * act, axis=0, keepdims=True
                )
            trace_row[0:1] = total

    w_copy = pltpu.make_async_copy(weights, w_vm, g_sem.at[nb])
    a_copy = pltpu.make_async_copy(acts, a_vm, g_sem.at[nb + 1])
    w_copy.start()
    a_copy.start()
    for b in range(nb):
        gram_copy(lax.rem(row + b, nb)).start()
    barrier = pltpu.get_barrier_semaphore()

    @pl.loop(1, members)
    def _(i):
        friend = lax.rem(me + i, members)
        pl.semaphore_signal(
            barrier, inc=1, device_id=(group, friend // 2, lax.rem(friend, 2)), device_id_type=MESH
        )

    w_copy.wait()
    for i in range(blocks):
        at = pl.ds(i * BLK, BLK)
        w = w_vm[at]
        put_own(0, at, (mask_at(i) * w - w).astype(jnp.bfloat16))
    a_copy.wait()
    own_inner(0)
    pl.semaphore_wait(barrier, members - 1)
    start_inner(0)

    @pl.when(col == 0)
    def _():
        for j in range(chunks):
            launch(0, j)

    y_acc[...] = jnp.zeros_like(y_acc)

    @pl.when(col == 1)
    def _():
        for j in range(chunks):
            launch(1, j)

    def owned(part, action, *rest):
        @pl.when(col == part % 2)
        def _():
            action(*rest)

    for phase in range(2):
        a, b = 2 * phase, 2 * phase + 1
        if phase == 1:
            owned(1, turn, 1)
        pass_on(a, 0, 0)
        owned(a, reduce_inner, phase, 0)
        if phase == 0:
            owned(b, reduce_inner, phase, 0)
            pass_on(b, 0, 0)
            a_turned[...] = a_vm[...].T
        pass_on(a, 0, 1)
        owned(a, reduce_inner, phase, 1)
        if phase == 0:
            for k in range(nb):
                gram_copy(lax.rem(row + k, nb)).wait()
            trace()
        else:
            pass_on(b, 0, 0)
            owned(b, reduce_inner, phase, 0)
        pass_on(b, 0, 1)
        owned(b, reduce_inner, phase, 1)
        process_self(phase)
        pass_on(a, 1, 0)
        process_both(phase, 0, 0)
        pass_on(b, 1, 0)
        process_both(phase, 1, 0)
        pass_on(a, 1, 1)
        owned(a, reduce_inner, phase, 2)
        pass_on(b, 1, 1)
        owned(b, reduce_inner, phase, 2)
        process_both(phase, 0, 1)
        pass_on(a, 2, 0)
        process_both(phase, 1, 1)
        pass_on(b, 2, 0)
        process_chunk(phase, 0, 2, 0)
        pass_on(a, 2, 1)
        process_chunk(phase, 1, 2, 0)
        pass_on(b, 2, 1)
        owned(a, add_update, a)
        process_chunk(phase, 0, 2, 1)
        process_chunk(phase, 1, 2, 1)
        if phase == 0:
            process_far(a)
            owned(a, turn, a)
            owned(b, add_update, b)
            process_far(b)
        else:
            owned(b, add_update, b)
            process_far_both(phase)
            owned(a, finish, a)

    owned(3, finish, 3)

    tot_all().wait_recv()

    totals = jnp.sum(jnp.sum(tot[...], axis=0), axis=1, keepdims=True)
    grad_square, grad_curve, curve_square, trace_total = (totals[i:i + 1] for i in range(4))
    damping = damping_ratio * trace_total / (n * rows)
    step_first = grad_square / (grad_curve + damping * grad_square + epsilon)
    step_second = (grad_curve + damping * grad_square) / (
        curve_square + 2.0 * damping * grad_curve + damping * damping * grad_square + epsilon
    )

    shape = (BLK, width)
    first = jnp.broadcast_to(step_first, shape)
    second = jnp.broadcast_to(step_second, shape)

    @pl.loop(0, blocks)
    def _(i):
        at = pl.ds(pl.multiple_of(i * BLK, BLK), BLK)
        gradient = grad[at]
        moved = w_vm[at] - first * gradient - second * (gradient - first * y_acc[2 + col, at])
        out[at] = mask_at(i) * moved

    for part in range(4):
        @pl.when(col == part % 2)
        def _():
            ring_sent(part, 0, 0).wait_send()
            ring_sent(part, 1, 0).wait_send()

            @pl.when(near_half != col)
            def _():
                for j in range(chunks):
                    to_partner(part, j).wait_send()

        @pl.when(col != part % 2)
        def _():
            for j in range(chunks):
                y_copy(part, j).wait_send()

        for way in range(2):
            for hop in range(1, last + 1):
                @pl.when(here(source_of(way, hop)))
                def _():
                    if hop < last:
                        ring_sent(part, way, hop).wait_send()
                    else:
                        for j in range(chunks):
                            if (j < split) == (way == 0):
                                ring(part, way, hop, j).wait_send()
    for phase in range(2):
        @pl.when(outer)
        def _():
            red_copy(phase, 0).wait_send()

        @pl.when(jnp.logical_not(outer))
        def _():
            for step in range(1, 4):
                red_copy(phase, step).wait_send()

    tot_all().wait_send()


def fused_device(gram_old, activations, weights, block_mask):
    n = lax.axis_size("row")
    rows, width = weights.shape
    depth = activations.shape[0]
    nb = gram_old.shape[1] // rows
    chunks = CUTS
    hops = n // 2
    low, wide = jnp.bfloat16, jnp.float32
    dma = pltpu.SemaphoreType.DMA
    return pl.pallas_call(
        functools.partial(fused_kernel, n),
        out_shape=jax.ShapeDtypeStruct((rows, width), wide),
        in_specs=[
            pl.BlockSpec(memory_space=pl.ANY),
            pl.BlockSpec(memory_space=pl.ANY),
            pl.BlockSpec(memory_space=pl.ANY),
            pl.BlockSpec(memory_space=pltpu.SMEM),
        ],
        out_specs=pl.BlockSpec(memory_space=pltpu.VMEM),
        scratch_shapes=[
            pltpu.VMEM((nb, rows, rows), low),
            pltpu.VMEM((2, rows, width), low),
            pltpu.VMEM((4, nb, rows, width), low),
            pltpu.VMEM((4, rows, width), wide),
            pltpu.VMEM((2, rows, width), wide),
            pltpu.VMEM((rows, width), wide),
            pltpu.VMEM((rows, width), wide),
            pltpu.VMEM((depth, rows), low),
            pltpu.VMEM((rows, depth), low),
            pltpu.VMEM((2, 4, depth, width), low),
            pltpu.VMEM((2, 4, depth, width), low),
            pltpu.VMEM((2, 3, depth, width), wide),
            pltpu.VMEM((8, width), wide),
            pltpu.VMEM((2 * n, 8, width), wide),
            dma((nb + 2,)),
            dma((4, 2, hops)),
            dma((4, 2, hops, chunks)),
            dma((4, chunks)),
            dma((4, chunks)),
            dma((2, chunks)),
            dma((2, chunks)),
            dma((2, 4)),
            dma((2, 4)),
            dma((2,)),
        ],
        compiler_params=pltpu.CompilerParams(
            collective_id=0, has_side_effects=True, vmem_limit_bytes=56 * 1024 * 1024
        ),
        name="fused_steps",
    )(gram_old, activations, weights, block_mask.T)


def fits(gram_old, activations, weights, n):
    rows, width = weights.shape
    return (
        rows % (CUTS * BLK) == 0
        and width == BLK
        and n == 8
        and gram_old.shape[1] == rows * n // 2
        and activations.shape[0] % BLK == 0
        and gram_old.size <= 14 * 1024 * 1024
    )


def one_device(gram_old, activations, weights, block_mask):
    if fits(gram_old, activations, weights, lax.axis_size("row")):
        return fused_device(gram_old, activations, weights, block_mask)
    return per_device(gram_old, activations, weights, block_mask)


def solution(mesh):
    placed = (
        P(("groups", "row"), "col"),
        P("groups", "row"),
        P("row", ("groups", "col")),
        P(None, "groups"),
    )
    return jax.shard_map(
        one_device,
        mesh=mesh,
        in_specs=placed,
        out_specs=P("row", ("groups", "col")),
        check_vma=False,
    )
```
